32 devices in a mesh: groups: 2 (over x), row: 8 (over z, y), col: 2 (over core).
Axes of the slice: x: 2, y: 2, z: 4, core: 2. Of those that a mesh axis runs over, the one named last changes fastest.
Arguments:
- queries: bfloat16 [512, 32, 128], P(('groups', 'row', 'col')), parts along dimension 0, may hold values from -4 to 4
- clauses: bfloat16 [512, 32, 128], P(('groups', 'row', 'col')), parts along dimension 0, may hold values from -4 to 4
- pattern: int32 [32, 16], P('groups'), parts along dimension 0, may hold values from 0 to 1, as said below
- positive: int32 [512], P(('groups', 'row', 'col')), parts along dimension 0, may hold values from 0 to 255, as said below
Outputs:
- per_query: float32 [512], P(('groups', 'row', 'col')), parts along dimension 0
- grad_queries: float32 [512, 32, 128], P(('groups', 'row', 'col')), parts along dimension 0
- grad_clauses: float32 [512, 32, 128], P(('groups', 'row', 'col')), parts along dimension 0
The draws below stay inside these ranges and needn't reach their ends.
There are 2 independent parts, one for each index of `groups`. The reference program is written for one: setup_inputs(seed, part) draws one part's arguments, and reference() takes and returns one part's arrays. A program takes and returns all parts, laid end to end along the dimension named above; each array names one. Nothing has to cross between parts.
Inputs may be any that keep to these rules, and one draw needn't show every extreme that they name: Block a holds rows a * 16 to a * 16 + 15; pattern[a, a] = 1 for every block a. positive is a permutation of the rows, and positive[i] lies in the same block of 16 rows as i.
All inputs are finite; a program needn't handle non-finite values.
Results may differ from the reference program's by a relative error of at most 0.0027.
Values may be sent and summed in bfloat16 or wider, within the bound.
A program may use at most 64 MiB of HBM per device.

```python
import jax
import jax.numpy as jnp
from jax import lax

E = 128
LQ = 32
LC = 32
QDEV = 16
NQ = 256


def draw_pair(key):
    draw_key = jax.random.fold_in(key, 17)
    query_key, clause_key = jax.random.split(draw_key, 2)
    query_draw = jnp.clip(0.35 * jax.random.normal(query_key, (NQ, LQ, E), jnp.float32), -4.0, 4.0)
    clause_draw = jnp.clip(0.35 * jax.random.normal(clause_key, (NQ, LC, E), jnp.float32), -4.0, 4.0)
    return (query_draw, clause_draw)


def draw_queries(key, part):
    return draw_pair(key)[0].astype(jnp.bfloat16)


def draw_clauses(key, part):
    return draw_pair(key)[1].astype(jnp.bfloat16)


def draw_pattern(key, part):
    block_total = NQ // QDEV
    density_key, ticket_key = jax.random.split(jax.random.fold_in(key, 5))
    density = jax.random.randint(density_key, (block_total, 1), 1, 8)
    ticket = jax.random.randint(ticket_key, (block_total, block_total), 0, 16)
    diagonal = jnp.arange(block_total)[:, None] == jnp.arange(block_total)[None, :]
    return jnp.where((ticket < density) | diagonal, 1, 0).astype(jnp.int32)


def draw_positive(key, part):
    block_total = NQ // QDEV
    block_keys = jax.random.split(jax.random.fold_in(key, 11), block_total)
    shuffles = jax.vmap(lambda block_key: jax.random.permutation(block_key, QDEV))(block_keys)
    offsets = jnp.arange(block_total, dtype=jnp.int32)[:, None] * QDEV
    return (shuffles.astype(jnp.int32) + offsets).reshape(NQ).astype(jnp.int32)


def setup_inputs(seed: int = 0, part: int = 0) -> dict:
    seeds = jax.random.split(jax.random.key(seed), 5)
    part_splits = jax.random.split(jax.random.fold_in(seeds[4], part), 5)
    return {
        "queries": draw_queries(jax.random.fold_in(jax.random.fold_in(seeds[4], part), 71), part),
        "clauses": draw_clauses(jax.random.fold_in(jax.random.fold_in(seeds[4], part), 71), part),
        "pattern": draw_pattern(jax.random.fold_in(jax.random.fold_in(seeds[4], part), 71), part),
        "positive": draw_positive(jax.random.fold_in(jax.random.fold_in(seeds[4], part), 71), part),
    }


SHARPNESS = 3.0
FLOOR_VALUE = -1.0e30


def tile_logits(query_tile, clause_tile):
    query_count, query_len, width_feat = query_tile.shape
    clause_count, clause_len = clause_tile.shape[0], clause_tile.shape[1]
    products = lax.dot_general(query_tile.reshape(query_count * query_len, width_feat),
                               clause_tile.reshape(clause_count * clause_len, width_feat),
                               (((1,), (1,)), ((), ())), preferred_element_type=jnp.float32)
    return (products * SHARPNESS).reshape(query_count, query_len, clause_count, clause_len)


def token_lse_of(logits):
    token_summit = jnp.max(logits, axis=3)
    return token_summit + jnp.log(jnp.sum(jnp.exp(logits - token_summit[..., None]), axis=3))


def tile_score(query_tile, clause_tile):
    return jnp.sum(token_lse_of(tile_logits(query_tile, clause_tile)), axis=1) / SHARPNESS


def tile_grads(query_tile, clause_tile, factor_tile):
    logits = tile_logits(query_tile, clause_tile)
    token_lse = token_lse_of(logits)
    weights = jnp.exp(logits - token_lse[..., None]) * factor_tile[:, None, :, None]
    query_count, query_len, width_feat = query_tile.shape
    clause_count, clause_len = clause_tile.shape[0], clause_tile.shape[1]
    weights = weights.reshape(query_count * query_len, clause_count * clause_len).astype(jnp.bfloat16)
    grad_query = jnp.dot(weights, clause_tile.reshape(clause_count * clause_len, width_feat),
                         preferred_element_type=jnp.float32)
    grad_clause = lax.dot_general(weights, query_tile.reshape(query_count * query_len, width_feat),
                                  (((0,), (0,)), ((), ())), preferred_element_type=jnp.float32)
    return grad_query.reshape(query_tile.shape), grad_clause.reshape(clause_tile.shape)


def masked_lse(masked, scored, along):
    summit = jnp.max(masked, axis=along, keepdims=True)
    amount = jnp.sum(jnp.where(scored, jnp.exp(masked - summit), 0.0), axis=along)
    return jnp.squeeze(summit, along) + jnp.log(amount)


def reference(queries, clauses, pattern, positive):
    total_rows = queries.shape[0]
    block_count = pattern.shape[0]
    block_rows = total_rows // block_count
    query_blocks = queries.reshape(block_count, block_rows, queries.shape[1], queries.shape[2])
    clause_blocks = clauses.reshape(block_count, block_rows, clauses.shape[1], clauses.shape[2])
    empty_tile = jnp.zeros((block_rows, block_rows), jnp.float32)

    def score_line(query_index):
        def visit_column(clause_index, score_line_rows):
            score_tile = lax.cond(pattern[query_index, clause_index] > 0,
                                  lambda: tile_score(query_blocks[query_index], clause_blocks[clause_index]),
                                  lambda: empty_tile)
            start_col = (clause_index * block_rows).astype(jnp.int32)
            return lax.dynamic_update_slice(score_line_rows, score_tile, (jnp.int32(0), start_col))
        return lax.fori_loop(0, block_count, visit_column, jnp.zeros((block_rows, total_rows), jnp.float32))

    scores = lax.map(score_line, jnp.arange(block_count, dtype=jnp.int32)).reshape(total_rows, total_rows)
    scored = jnp.repeat(jnp.repeat(pattern > 0, block_rows, axis=0), block_rows, axis=1)
    masked = jnp.where(scored, scores, FLOOR_VALUE)
    row_lse = masked_lse(masked, scored, 1)
    col_lse = masked_lse(masked, scored, 0)
    clause_index_all = jnp.arange(total_rows, dtype=jnp.int32)
    matches = positive[:, None] == clause_index_all[None, :]
    positive_score = jnp.sum(jnp.where(matches, scores, 0.0), axis=1)
    positive_col = jnp.sum(jnp.where(matches, col_lse[None, :], 0.0), axis=1)
    per_query = 0.5 * (row_lse - positive_score) + 0.5 * (positive_col - positive_score)
    factor = 0.5 * (jnp.exp(masked - row_lse[:, None]) + jnp.exp(masked - col_lse[None, :])) - jnp.where(matches, 1.0, 0.0)

    def grad_line(query_index, running):
        grad_queries, grad_clauses = running
        query_tile = query_blocks[query_index]
        start_row = (query_index * block_rows).astype(jnp.int32)

        def visit_column(clause_index, running_pair):
            line_grad, clause_grads = running_pair
            start_col = (clause_index * block_rows).astype(jnp.int32)
            factor_tile = lax.dynamic_slice(factor, (start_row, start_col), (block_rows, block_rows))
            clause_tile = clause_blocks[clause_index]
            query_part, clause_part = lax.cond(
                pattern[query_index, clause_index] > 0,
                lambda: tile_grads(query_tile, clause_tile, factor_tile),
                lambda: (jnp.zeros(query_tile.shape, jnp.float32), jnp.zeros(clause_tile.shape, jnp.float32)))
            current = lax.dynamic_slice_in_dim(clause_grads, start_col, block_rows, 0)
            clause_grads = lax.dynamic_update_slice_in_dim(clause_grads, current + clause_part, start_col, 0)
            return line_grad + query_part, clause_grads

        line_grad, grad_clauses = lax.fori_loop(0, block_count, visit_column,
                                                (jnp.zeros(query_tile.shape, jnp.float32), grad_clauses))
        grad_queries = lax.dynamic_update_slice_in_dim(grad_queries, line_grad, start_row, 0)
        return grad_queries, grad_clauses

    grad_queries, grad_clauses = lax.fori_loop(
        0, block_count, grad_line,
        (jnp.zeros(queries.shape, jnp.float32), jnp.zeros(clauses.shape, jnp.float32)))
    return (per_query, grad_queries, grad_clauses)
```

```python
import functools
import math

import jax
import jax.numpy as jnp
from jax import lax
from jax.experimental import pallas as pl
from jax.experimental.pallas import tpu as pltpu
from jax.sharding import PartitionSpec as P

SHARPNESS = 3.0
FLOOR_VALUE = -1e30
EXP2_SCALE = SHARPNESS * math.log2(math.e)
F32 = jnp.float32
BF16 = jnp.bfloat16
MESH = pl.DeviceIdType.MESH
LANES = 128
SUBLANES = 8
SQUARE = 4
NEXT, OVER, CORNER = 1, 2, 3
HALVES = 2


def dot(a, b, dims):
    return lax.dot_general(a, b, (dims, ((), ())), preferred_element_type=F32)


def roll_all(x, op, shifts):
    for shift in shifts:
        x = op(x, pltpu.roll(x, shift, 1))
    return x


def lse_of(top, total):
    return top + jnp.log(total)


def kernel(
    dims, far_count, q_hbm, c_hbm, pattern_hbm, positive_hbm,
    per_query_ref, grad_q_ref, grad_c_ref,
    stage, wide, qs, cs, raised, inverse, scores, row_stats, col_stats, factors, weights, sum_q, sum_c,
    out_sib_far, out_far, out_sib, out_next, out_corner, out_over,
    in_sib_far, in_far, in_sib, in_next, in_corner, in_over,
    pattern_ref, positive_ref, local_sem, gather_send, gather_recv, stats_send, stats_recv, grad_send, grad_recv,
):
    block, length, width = dims
    tokens = block * length
    half = tokens // HALVES
    groups = block // SUBLANES
    places = 2 * far_count
    row, core = lax.axis_index("row"), lax.axis_index("col")
    a, b = row // SQUARE, row % SQUARE
    mine = a * 2 + core

    def square(bits):
        high, low = b // 2, b % 2
        high = 1 - high if bits & OVER else high
        low = 1 - low if bits & NEXT else low
        return high * 2 + low

    def square_device(bits):
        return {"row": a * SQUARE + square(bits), "col": core}

    def far_row(step):
        return (a + step) % far_count

    def far_device(step, other):
        return {"row": far_row(step) * SQUARE + b, "col": 1 - core if other else core}

    def place(step, other):
        return far_row(step) * 2 + (1 - core if other else core)

    sibling = {"col": 1 - core}
    q_peers = [(step, other) for step in range(far_count) for other in (0, 1) if step or other]
    c_peers = [NEXT, OVER, CORNER]

    def remote(src, dst, send, recv, device):
        return pltpu.make_async_remote_copy(
            src_ref=src, dst_ref=dst, send_sem=send, recv_sem=recv, device_id=device, device_id_type=MESH
        )

    barrier = pltpu.get_barrier_semaphore()
    for step, other in q_peers:
        pl.semaphore_signal(barrier, inc=1, device_id=far_device(step, other), device_id_type=MESH)
    for bits in c_peers:
        pl.semaphore_signal(barrier, inc=1, device_id=square_device(bits), device_id_type=MESH)
    loads = [
        pltpu.make_async_copy(c_hbm, stage.at[0], local_sem.at[0]),
        pltpu.make_async_copy(q_hbm, stage.at[1], local_sem.at[1]),
        pltpu.make_async_copy(pattern_hbm, pattern_ref, local_sem.at[2]),
        pltpu.make_async_copy(positive_hbm, positive_ref, local_sem.at[3]),
    ]
    for load in loads:
        load.start()

    loads[0].wait()
    wide[...] = stage[0].astype(F32)
    for g in range(groups):
        for u in range(0, length, 2):
            pair = [wide[pl.ds(g * SUBLANES * length + u + k, SUBLANES, stride=length), :] for k in (0, 1)]
            cs[b, pl.ds((g * length + u) * SUBLANES, 2 * SUBLANES), :] = jnp.concatenate(pair, axis=0).astype(BF16)
    loads[1].wait()
    wide[...] = stage[1].astype(F32)
    for t in range(length):
        qs[mine, pl.ds(t * block, block), :] = wide[pl.ds(t, block, stride=length), :].astype(BF16)
    pl.semaphore_wait(barrier, len(q_peers) + len(c_peers))

    def part(h):
        return pl.ds(h * half, half)

    def send_c(index, source, bits, h):
        rows = part(h)
        return remote(
            cs.at[source, rows, :], cs.at[source, rows, :],
            gather_send.at[index, h], gather_recv.at[index, h], square_device(bits),
        )

    def send_q(index, source, device, h):
        rows = part(h)
        return remote(
            qs.at[source, rows, :], qs.at[source, rows, :], gather_send.at[index, h], gather_recv.at[index, h], device
        )

    def c_over(h):
        return send_c(0, b, OVER, h)

    def c_next(h):
        return send_c(1, b, NEXT, h)

    def c_corner(h):
        return send_c(2, square(OVER), NEXT, h)

    def q_sib(h):
        return send_q(3, mine, sibling, h)

    def q_far(step, h):
        return send_q(3 + step, mine, far_device(far_count - step, 0), h)

    def q_far_sib(step, h):
        return send_q(2 + far_count + step, place(step, 0), sibling, h)

    def got_q_far(step, h):
        return q_far(step, h)

    def score(c_place, q_place):
        total_lse = [None] * groups
        for lane in range(tokens // LANES):
            lanes = pl.ds(lane * LANES, LANES)
            for g in range(groups):
                rows = pl.ds(g * SUBLANES * length, SUBLANES * length)
                logits = dot(cs[c_place, rows, :], qs[q_place, lanes, :], ((1,), (1,))).reshape(length, SUBLANES, LANES)
                top = jnp.max(logits, axis=0)
                exps = jnp.exp2((logits - top[None]) * EXP2_SCALE)
                total = jnp.sum(exps, axis=0)
                raised[c_place, q_place, rows, lanes] = exps.reshape(SUBLANES * length, LANES)
                inverse[c_place, q_place, pl.ds(g * SUBLANES, SUBLANES), lanes] = 1.0 / total
                lse = top * SHARPNESS + jnp.log(total)
                total_lse[g] = lse if total_lse[g] is None else total_lse[g] + lse
        full = jnp.concatenate(total_lse, axis=0)
        shifts = [block * 2**k for k in range(int(math.log2(LANES // block)))]
        scores[c_place, q_place] = roll_all(full, jnp.add, shifts) / SHARPNESS

    for h in range(HALVES):
        c_over(h).start()
        for step in range(1, far_count):
            q_far(step, h).start()
        c_next(h).start()
        q_sib(h).start()
    score(b, mine)
    for h in range(HALVES):
        q_sib(h).wait_recv()
    score(b, place(0, 1))
    for h in range(HALVES):
        c_over(h).wait_recv()
        c_corner(h).start()
    for other in (0, 1):
        score(square(OVER), place(0, other))
    for h in range(HALVES):
        c_next(h).wait_recv()
    for other in (0, 1):
        score(square(NEXT), place(0, other))
    for step in range(1, far_count):
        for h in range(HALVES):
            got_q_far(step, h).wait_recv()
            q_far_sib(step, h).start()
        for bits in (0, OVER, NEXT):
            score(square(bits), place(step, 0))
    for step in range(1, far_count):
        for h in range(HALVES):
            q_far_sib(step, h).wait_recv()
        for bits in (0, OVER, NEXT):
            score(square(bits), place(step, 1))
    for h in range(HALVES):
        c_corner(h).wait_recv()
    for step in range(far_count):
        for other in (0, 1):
            score(square(CORNER), place(step, other))

    loads[2].wait()
    loads[3].wait()
    tile = (block, LANES)

    def masked(k, p):
        query_block = ((p // 2) * SQUARE + b) * 2 + p % 2
        clause_block = (a * SQUARE + k) * 2 + core
        scored = jnp.full(tile, pattern_ref[query_block, clause_block], jnp.int32) > 0
        return jnp.where(scored, scores[k, p], FLOOR_VALUE)

    tiles = [[masked(k, p) for p in range(places)] for k in range(SQUARE)]
    tops, sums = [], []
    for p in range(places):
        column = [tiles[k][p] for k in range(SQUARE)]
        top = jnp.max(functools.reduce(jnp.maximum, column), axis=0, keepdims=True)
        tops.append(top)
        sums.append(jnp.sum(sum(jnp.exp(x - top) for x in column), axis=0, keepdims=True))
    row_stats[mine] = jnp.concatenate(tops + sums, axis=0)

    def send_rows(index, step, other):
        return remote(
            row_stats.at[mine], row_stats.at[mine], stats_send.at[index], stats_recv.at[index], far_device(step, other)
        )

    def send_cols(index, bits):
        return remote(
            col_stats.at[b], col_stats.at[b], stats_send.at[index], stats_recv.at[index], square_device(bits)
        )

    stat_copies = []
    for step, other in q_peers:
        stat_copies.append(send_rows(len(stat_copies), step, other))
        stat_copies[-1].start()

    lane_group = lax.broadcasted_iota(jnp.int32, (SUBLANES, LANES), 1) // block
    shifts = [2**k for k in range(int(math.log2(block)))]
    top_pack = jnp.zeros((SUBLANES, LANES), F32)
    sum_pack = jnp.ones((SUBLANES, LANES), F32)
    for k in range(SQUARE):
        top = roll_all(functools.reduce(jnp.maximum, tiles[k]), jnp.maximum, shifts)
        total = roll_all(sum(jnp.exp(x - top) for x in tiles[k]), jnp.add, shifts)
        for g in range(groups):
            here = lane_group == k * groups + g
            rows = slice(g * SUBLANES, (g + 1) * SUBLANES)
            top_pack = jnp.where(here, top[rows], top_pack)
            sum_pack = jnp.where(here, total[rows], sum_pack)
    col_stats[b] = jnp.concatenate([top_pack, sum_pack], axis=0)
    for bits in c_peers:
        stat_copies.append(send_cols(len(stat_copies), bits))
        stat_copies[-1].start()
    for copy in stat_copies:
        copy.wait_recv()

    def combine(stats, count, rows):
        top = functools.reduce(jnp.maximum, [stats[s, pl.ds(0, rows), :] for s in range(count)])
        total = sum(
            stats[s, pl.ds(rows, rows), :] * jnp.exp(stats[s, pl.ds(0, rows), :] - top) for s in range(count)
        )
        return lse_of(top, total)

    row_lse = combine(row_stats, places, places)
    col_pack = combine(col_stats, SQUARE, SUBLANES)
    row_of = [jnp.broadcast_to(row_lse[p : p + 1], tile) for p in range(places)]
    col_of = []
    for k in range(SQUARE):
        parts = []
        for g in range(groups):
            at = (k * groups + g) * block
            parts.append(jnp.broadcast_to(col_pack[:, at : at + 1], (SUBLANES, LANES)))
        col_of.append(jnp.concatenate(parts, axis=0))
    for k in range(SQUARE):
        for p in range(places):
            x = tiles[k][p]
            factors[k, p] = 0.5 * (jnp.exp(x - row_of[p]) + jnp.exp(x - col_of[k]))

    item = lax.broadcasted_iota(jnp.int32, tile, 1) % block
    positive = jnp.zeros(tile, jnp.int32)
    for i in range(block):
        positive = jnp.where(item == i, positive_ref[i], positive)
    own_first = (row * 2 + core) * block
    matches = positive - own_first == lax.broadcasted_iota(jnp.int32, tile, 0)
    own_row = jnp.zeros((1, LANES), F32)
    own_col = jnp.zeros(tile, F32)
    for p in range(places):
        own_row = jnp.where(mine == p, row_lse[p : p + 1], own_row)
    for k in range(SQUARE):
        own_col = jnp.where(b == k, col_of[k], own_col)
    positive_score = jnp.sum(jnp.where(matches, scores[b, mine], 0.0), axis=0, keepdims=True)
    positive_col = jnp.sum(jnp.where(matches, own_col, 0.0), axis=0, keepdims=True)
    per_query_ref[...] = 0.5 * (own_row - positive_score) + 0.5 * (positive_col - positive_score)
    factors[b, mine] = factors[b, mine] - jnp.where(matches, 1.0, 0.0)

    def weigh(slot, k, p):
        for lane in range(tokens // LANES):
            lanes = pl.ds(lane * LANES, LANES)
            for g in range(groups):
                rows = pl.ds(g * SUBLANES * length, SUBLANES * length)
                few = pl.ds(g * SUBLANES, SUBLANES)
                scale = factors[k, p, few, :] * inverse[k, p, few, lanes]
                exps = raised[k, p, rows, lanes].reshape(length, SUBLANES, LANES)
                weights[slot, rows, lanes] = (exps * scale[None]).reshape(SUBLANES * length, LANES).astype(BF16)

    seen_q, seen_c = set(), set()

    def grads(pairs):
        for slot, (bits, step, other) in enumerate(pairs):
            k, p = square(bits), place(step, other)
            weigh(slot, k, p)
            to_q = dot(cs[k], weights[slot], ((0,), (0,)))
            to_c = dot(weights[slot], qs[p], ((1,), (0,)))
            if (step, other) in seen_q:
                sum_q[p] += to_q
            else:
                sum_q[p] = to_q
            if bits in seen_c:
                sum_c[k] += to_c
            else:
                sum_c[k] = to_c
            seen_q.add((step, other))
            seen_c.add(bits)

    def grad_copy(index, src, dst, device, h=0):
        return remote(src, dst, grad_send.at[index, h], grad_recv.at[index, h], device)

    def g_sib():
        return grad_copy(0, out_sib, in_sib, sibling)

    def g_next():
        return grad_copy(1, out_next, in_next, square_device(NEXT))

    def g_corner(h):
        return grad_copy(2, out_corner.at[part(h), :], in_corner.at[part(h), :], square_device(NEXT), h)

    def g_over(h):
        return grad_copy(3, out_over.at[part(h), :], in_over.at[part(h), :], square_device(OVER), h)

    def g_sib_far(step):
        return grad_copy(3 + step, out_sib_far.at[step - 1], in_sib_far.at[step - 1], sibling)

    def g_far(step):
        return grad_copy(2 + far_count + step, out_far.at[step - 1], in_far.at[step - 1], far_device(step, 0))

    order = (CORNER, NEXT, OVER, 0)
    for step in range(1, far_count):
        grads([(bits, step, 1) for bits in order])
        out_sib_far[step - 1] = sum_q[place(step, 1)].astype(BF16)
        g_sib_far(step).start()
        grads([(bits, step, 0) for bits in order])
        g_sib_far(step).wait_recv()
        out_far[step - 1] = (sum_q[place(step, 0)] + in_sib_far[step - 1].astype(F32)).astype(BF16)
        g_far(step).start()
    grads([(CORNER, 0, 1), (CORNER, 0, 0)])
    for h in range(HALVES):
        out_corner[part(h), :] = sum_c[square(CORNER), part(h), :].astype(BF16)
        g_corner(h).start()
    grads([(NEXT, 0, 1), (NEXT, 0, 0)])
    out_next[...] = sum_c[square(NEXT)].astype(BF16)
    g_next().start()
    grads([(OVER, 0, 1), (OVER, 0, 0)])
    grads([(0, 0, 1)])
    out_sib[...] = sum_q[place(0, 1)].astype(BF16)
    g_sib().start()
    grads([(0, 0, 0)])
    for h in range(HALVES):
        g_corner(h).wait_recv()
        out_over[part(h), :] = (sum_c[square(OVER), part(h), :] + in_corner[part(h), :].astype(F32)).astype(BF16)
        g_over(h).start()

    g_sib().wait_recv()
    total_q = sum_q[mine] + in_sib[...].astype(F32)
    for step in range(1, far_count):
        g_far(step).wait_recv()
        total_q = total_q + in_far[step - 1].astype(F32)
    wide[...] = total_q.T
    for i in range(block):
        grad_q_ref[pl.ds(i * length, length), :] = wide[pl.ds(i, length, stride=block), :]

    g_next().wait_recv()
    sum_c[b] += in_next[...].astype(F32)
    for h in range(HALVES):
        g_over(h).wait_recv()
        wide[part(h), :] = sum_c[b, part(h), :] + in_over[part(h), :].astype(F32)
    for j in range(block):
        start = (j // SUBLANES) * SUBLANES * length + j % SUBLANES
        grad_c_ref[pl.ds(j * length, length), :] = wide[pl.ds(start, length, stride=SUBLANES), :]

    for h in range(HALVES):
        for copy in (c_over(h), c_next(h), c_corner(h), q_sib(h), g_corner(h), g_over(h)):
            copy.wait_send()
        for step in range(1, far_count):
            q_far(step, h).wait_send()
            q_far_sib(step, h).wait_send()
    for copy in stat_copies:
        copy.wait_send()
    g_sib().wait_send()
    g_next().wait_send()
    for step in range(1, far_count):
        g_sib_far(step).wait_send()
        g_far(step).wait_send()


def shards(queries, clauses, pattern, positive):
    block, length, width = queries.shape
    tokens = block * length
    far_count = lax.axis_size("row") // SQUARE
    places = 2 * far_count
    far = max(far_count - 1, 1)
    vmem = pl.BlockSpec(memory_space=pltpu.VMEM)
    hbm = pl.BlockSpec(memory_space=pltpu.HBM)
    sems = pltpu.SemaphoreType.DMA
    V = pltpu.VMEM
    per_query, grad_q, grad_c = pl.pallas_call(
        functools.partial(kernel, (block, length, width), far_count),
        out_shape=(
            jax.ShapeDtypeStruct((1, LANES), F32),
            jax.ShapeDtypeStruct((tokens, width), F32),
            jax.ShapeDtypeStruct((tokens, width), F32),
        ),
        in_specs=[hbm] * 4,
        out_specs=(vmem, vmem, vmem),
        scratch_shapes=[
            V((2, tokens, width), BF16),
            V((tokens, width), F32),
            V((places, tokens, width), BF16),
            V((SQUARE, tokens, width), BF16),
            V((SQUARE, places, tokens, tokens), F32),
            V((SQUARE, places, block, tokens), F32),
            V((SQUARE, places, block, LANES), F32),
            V((places, 2 * places, LANES), F32),
            V((SQUARE, 2 * SUBLANES, LANES), F32),
            V((SQUARE, places, block, LANES), F32),
            V((4, tokens, tokens), BF16),
            V((places, width, tokens), F32),
            V((SQUARE, tokens, width), F32),
            V((far, width, tokens), BF16),
            V((far, width, tokens), BF16),
            V((width, tokens), BF16),
            V((tokens, width), BF16),
            V((tokens, width), BF16),
            V((tokens, width), BF16),
            V((far, width, tokens), BF16),
            V((far, width, tokens), BF16),
            V((width, tokens), BF16),
            V((tokens, width), BF16),
            V((tokens, width), BF16),
            V((tokens, width), BF16),
            pltpu.SMEM(pattern.shape, jnp.int32),
            pltpu.SMEM(positive.shape, jnp.int32),
            sems((4,)),
            sems((2 * far_count + 2, HALVES)),
            sems((2 * far_count + 2, HALVES)),
            sems((places + SQUARE - 2,)),
            sems((places + SQUARE - 2,)),
            sems((2 * far_count + 2, HALVES)),
            sems((2 * far_count + 2, HALVES)),
        ],
        compiler_params=pltpu.CompilerParams(
            collective_id=0, has_side_effects=True, vmem_limit_bytes=60 * 1024 * 1024
        ),
        name="contrastive",
    )(queries.reshape(tokens, width), clauses.reshape(tokens, width), pattern, positive)
    return (
        per_query[0, :block],
        grad_q.reshape(queries.shape),
        grad_c.reshape(clauses.shape),
    )


def solution(mesh):
    rows = P(("groups", "row", "col"), None, None)
    ids = P(("groups", "row", "col"))
    return jax.shard_map(
        shards,
        mesh=mesh,
        in_specs=(rows, rows, P("groups", None), ids),
        out_specs=(ids, rows, rows),
        check_vma=False,
    )
```

```python
import functools
import math

import jax
import jax.numpy as jnp
from jax import lax
from jax.experimental import pallas as pl
from jax.experimental.pallas import tpu as pltpu
from jax.sharding import PartitionSpec as P

SHARPNESS = 3.0
FLOOR_VALUE = -1e30
EXP2_SCALE = SHARPNESS * math.log2(math.e)
F32 = jnp.float32
BF16 = jnp.bfloat16
MESH = pl.DeviceIdType.MESH
LANES = 128
SUBLANES = 8
SQUARE = 4
NEXT, OVER, CORNER = 1, 2, 3
Q_PARTS, C_PARTS = 4, 2
GRAD_Q_PARTS, GRAD_C_PARTS = 1, 4


def dot(a, b, dims):
    return lax.dot_general(a, b, (dims, ((), ())), preferred_element_type=F32)


def swap(x, lane, bit):
    return jnp.take_along_axis(x, lane ^ bit, axis=1)


def spread(x, op, lane, bits):
    for bit in bits:
        x = op(x, swap(x, lane, bit))
    return x


def total_rows(x, op):
    for shift in (4, 2, 1):
        x = op(x, pltpu.roll(x, shift, 0))
    return x


def kernel(
    dims, far_count, q_hbm, c_hbm, pattern_hbm, positive_hbm,
    per_query_ref, grad_q_hbm, grad_c_hbm,
    stage, wide, qs, cs, cts, raised, inverse, lse_sums, packed, row_stats, col_stats, lses, factors, weights, sum_c, out_q, out_c,
    out_sib_far, out_far, out_next, out_corner, out_over, out_sib,
    in_sib_far, in_far, in_next, in_corner, in_over, in_sib,
    pattern_ref, positive_ref, local_sem, gather_send, gather_recv, stats_send, stats_recv, grad_send, grad_recv,
):
    block, length, width = dims
    tokens = block * length
    lane_tiles = tokens // LANES
    groups = block // SUBLANES
    places = 2 * far_count
    lse_rows = places + -places % SUBLANES
    row, core = lax.axis_index("row"), lax.axis_index("col")
    a, b = row // SQUARE, row % SQUARE
    mine = a * 2 + core

    def square(bits):
        high, low = b // 2, b % 2
        high = 1 - high if bits & OVER else high
        low = 1 - low if bits & NEXT else low
        return high * 2 + low

    def square_device(bits):
        return {"row": a * SQUARE + square(bits), "col": core}

    def far_row(step):
        return (a + step) % far_count

    def far_device(step, other):
        return {"row": far_row(step) * SQUARE + b, "col": 1 - core if other else core}

    def place(step, other):
        return far_row(step) * 2 + (1 - core if other else core)

    sibling = {"col": 1 - core}
    q_peers = [(step, other) for step in range(far_count) for other in (0, 1) if step or other]
    c_peers = [NEXT, OVER, CORNER]

    def remote(src, dst, send, recv, device):
        return pltpu.make_async_remote_copy(
            src_ref=src, dst_ref=dst, send_sem=send, recv_sem=recv, device_id=device, device_id_type=MESH
        )

    barrier = pltpu.get_barrier_semaphore()
    for step, other in q_peers:
        pl.semaphore_signal(barrier, inc=1, device_id=far_device(step, other), device_id_type=MESH)
    for bits in c_peers:
        pl.semaphore_signal(barrier, inc=1, device_id=square_device(bits), device_id_type=MESH)
    loads = [
        pltpu.make_async_copy(q_hbm, stage.at[0], local_sem.at[0]),
        pltpu.make_async_copy(c_hbm, stage.at[1], local_sem.at[1]),
        pltpu.make_async_copy(pattern_hbm, pattern_ref, local_sem.at[2]),
        pltpu.make_async_copy(positive_hbm, positive_ref, local_sem.at[3]),
    ]
    for load in loads:
        load.start()

    loads[0].wait()
    wide[0] = stage[0].astype(F32)
    for t in range(length):
        qs[mine, pl.ds(t * block, block), :] = wide[0, pl.ds(t, block, stride=length), :].astype(BF16)
    loads[1].wait()
    wide[1] = stage[1].astype(F32)
    for g in range(groups):
        for u in range(0, length, 2):
            pair = [wide[1, pl.ds(g * SUBLANES * length + u + k, SUBLANES, stride=length), :] for k in (0, 1)]
            cs[b, pl.ds((g * length + u) * SUBLANES, 2 * SUBLANES), :] = jnp.concatenate(pair, axis=0).astype(BF16)
    pl.semaphore_wait(barrier, len(q_peers) + len(c_peers))

    def part(h, parts):
        return pl.ds(h * (tokens // parts), tokens // parts)

    def send_c(index, source, bits, h):
        here = cs.at[source, part(h, C_PARTS), :]
        return remote(here, here, gather_send.at[index, h], gather_recv.at[index, h], square_device(bits))

    def send_q(index, source, device, h, parts):
        here = qs.at[source, part(h, parts), :]
        return remote(here, here, gather_send.at[index, h], gather_recv.at[index, h], device)

    def c_over(h):
        return send_c(0, b, OVER, h)

    def c_next(h):
        return send_c(1, b, NEXT, h)

    def c_corner(h):
        return send_c(2, square(OVER), NEXT, h)

    def q_sib():
        return send_q(3, mine, sibling, 0, 1)

    def q_far(step, h):
        return send_q(3 + step, mine, far_device(far_count - step, 0), h, Q_PARTS)

    def q_far_sib(step, h):
        return send_q(2 + far_count + step, place(step, 0), sibling, h, Q_PARTS)

    begun = set()

    def score(name, lanes, gs):
        bits, step, other = name
        c_place, q_place = square(bits), place(step, other)
        for lane in lanes:
            at = pl.ds(lane * LANES, LANES)
            for g in gs:
                rows = pl.ds(g * SUBLANES * length, SUBLANES * length)
                few = pl.ds(g * SUBLANES, SUBLANES)
                logits = dot(cs[c_place, rows, :], qs[q_place, at, :], ((1,), (1,))).reshape(length, SUBLANES, LANES)
                top = jnp.max(logits, axis=0)
                exps = jnp.exp2((logits - top[None]) * EXP2_SCALE)
                total = jnp.sum(exps, axis=0)
                raised[c_place, q_place, rows, at] = exps.reshape(SUBLANES * length, LANES)
                inverse[c_place, q_place, few, at] = 1.0 / total
                lse = top * SHARPNESS + jnp.log(total)
                if (name, g) in begun:
                    lse_sums[c_place, q_place, few, :] += lse
                else:
                    lse_sums[c_place, q_place, few, :] = lse
                    begun.add((name, g))

    all_lanes, all_groups = range(lane_tiles), range(groups)

    def lanes_of(h):
        return range(h * lane_tiles // Q_PARTS, (h + 1) * lane_tiles // Q_PARTS)

    def groups_of(h):
        return range(h * groups // C_PARTS, (h + 1) * groups // C_PARTS)

    for step in range(1, far_count):
        for h in range(Q_PARTS):
            q_far(step, h).start()
    for h in range(C_PARTS):
        c_over(h).start()
    q_sib().start()
    for h in range(C_PARTS):
        c_next(h).start()
    score((0, 0, 0), all_lanes, all_groups)
    cts[b] = cs[b].T

    loads[2].wait()
    loads[3].wait()
    pack_tile = (SUBLANES, LANES)
    lane = lax.broadcasted_iota(jnp.int32, pack_tile, 1)
    sublane = lax.broadcasted_iota(jnp.int32, pack_tile, 0)
    outer = [block << n for n in range(int(math.log2(LANES // block)))]
    inner = [1 << n for n in range(int(math.log2(block)))]

    def scored_lanes(p):
        query_block = ((p // 2) * SQUARE + b) * 2 + p % 2
        flags = jnp.zeros(pack_tile, jnp.int32)
        for k in range(SQUARE):
            first = k * groups * block
            here = (lane >= first) & (lane < first + groups * block)
            flags = jnp.where(here, pattern_ref[query_block, (a * SQUARE + k) * 2 + core], flags)
        return flags > 0

    scored = [scored_lanes(p) for p in range(places)]
    wanted = jnp.full(pack_tile, -1, jnp.int32)
    for i in range(block):
        wanted = jnp.where((lane & (block - 1)) == i, positive_ref[i], wanted)
    wanted = wanted - (row * 2 + core) * block
    for g in range(groups):
        first = (b * groups + g) * block
        here = (lane >= first) & (lane < first + block)
        found = here & (wanted == sublane + g * SUBLANES)
        matches = found if g == 0 else matches | found

    def pack(p):
        parts = [lse_sums[k, p, pl.ds(g * SUBLANES, SUBLANES), :] for k in range(SQUARE) for g in range(groups)]
        bit = LANES // 2
        while len(parts) > 1:
            low = (lane & bit) == 0
            count = len(parts) // 2
            parts = [
                jnp.where(low, x, y) + swap(jnp.where(low, y, x), lane, bit)
                for x, y in zip(parts[:count], parts[count:])
            ]
            bit //= 2
        return parts[0] / SHARPNESS

    q_sib().wait_recv()
    score((0, 0, 1), all_lanes, all_groups)
    for h in range(C_PARTS):
        c_over(h).wait_recv()
        c_corner(h).start()
        for other in (0, 1):
            score((OVER, 0, other), all_lanes, groups_of(h))
        c_next(h).wait_recv()
        for other in (0, 1):
            score((NEXT, 0, other), all_lanes, groups_of(h))
    cts[square(OVER)] = cs[square(OVER)].T
    cts[square(NEXT)] = cs[square(NEXT)].T
    near = (0, OVER, NEXT)
    for step in range(1, far_count):
        for h in range(Q_PARTS + 1):
            if h < Q_PARTS:
                q_far(step, h).wait_recv()
                q_far_sib(step, h).start()
                for bits in near:
                    score((bits, step, 0), lanes_of(h), all_groups)
            if h == Q_PARTS and step == far_count - 1:
                for g in range(C_PARTS - 1):
                    c_corner(g).wait_recv()
                    for s in range(far_count):
                        for other in (0, 1):
                            if s < step or other == 0:
                                score((CORNER, s, other), all_lanes, groups_of(g))
            if h:
                q_far_sib(step, h - 1).wait_recv()
                for bits in near:
                    score((bits, step, 1), lanes_of(h - 1), all_groups)
    for g in range(C_PARTS - 1):
        score((CORNER, far_count - 1, 1), all_lanes, groups_of(g))
    c_corner(C_PARTS - 1).wait_recv()
    for step in range(far_count):
        for other in (0, 1):
            score((CORNER, step, other), all_lanes, groups_of(C_PARTS - 1))

    for p in range(places):
        packed[p] = jnp.where(scored[p], pack(p), FLOOR_VALUE)
    values = [packed[p] for p in range(places)]
    tops, sums = [], []
    for x in values:
        top = spread(total_rows(x, jnp.maximum), jnp.maximum, lane, outer)
        tops.append(top[:1])
        sums.append(spread(total_rows(jnp.exp(x - top), jnp.add), jnp.add, lane, outer)[:1])
    row_stats[mine] = jnp.concatenate(tops + sums, axis=0)

    def send_rows(index, step, other):
        return remote(
            row_stats.at[mine], row_stats.at[mine], stats_send.at[index], stats_recv.at[index], far_device(step, other)
        )

    def send_cols(index, bits):
        return remote(
            col_stats.at[b], col_stats.at[b], stats_send.at[index], stats_recv.at[index], square_device(bits)
        )

    stat_copies = []
    for step, other in q_peers:
        stat_copies.append(send_rows(len(stat_copies), step, other))
        stat_copies[-1].start()
    top = spread(functools.reduce(jnp.maximum, values), jnp.maximum, lane, inner)
    total = spread(sum(jnp.exp(x - top) for x in values), jnp.add, lane, inner)
    col_stats[b] = jnp.concatenate([top, total], axis=0)
    for bits in c_peers:
        stat_copies.append(send_cols(len(stat_copies), bits))
        stat_copies[-1].start()
    cts[square(CORNER)] = cs[square(CORNER)].T
    for copy in stat_copies:
        copy.wait_recv()

    def combine(stats, count, rows):
        top = functools.reduce(jnp.maximum, [stats[s, pl.ds(0, rows), :] for s in range(count)])
        total = sum(
            stats[s, pl.ds(rows, rows), :] * jnp.exp(stats[s, pl.ds(0, rows), :] - top) for s in range(count)
        )
        return top + jnp.log(total)

    row_lse = combine(row_stats, places, places)
    col_lse = combine(col_stats, SQUARE, SUBLANES)
    for p in range(places):
        x = values[p]
        factors[p] = 0.5 * (jnp.exp(x - row_lse[p : p + 1]) + jnp.exp(x - col_lse))
    factors[mine] = factors[mine] - jnp.where(matches, 1.0, 0.0)
    lses[pl.ds(0, places), :] = row_lse
    lses[pl.ds(lse_rows, SUBLANES), :] = col_lse

    def factor_of(k, p, g):
        return jnp.take_along_axis(factors[p], (k * groups + g) * block + (lane & (block - 1)), axis=1)

    def weigh(bits, step, other, lanes):
        k, p = square(bits), place(step, other)
        for lane in lanes:
            at = pl.ds(lane * LANES, LANES)
            for g in range(groups):
                rows = pl.ds(g * SUBLANES * length, SUBLANES * length)
                few = pl.ds(g * SUBLANES, SUBLANES)
                scale = factor_of(k, p, g) * inverse[k, p, few, at]
                exps = raised[k, p, rows, at].reshape(length, SUBLANES, LANES)
                weights[k, p, rows, at] = (exps * scale[None]).reshape(SUBLANES * length, LANES).astype(BF16)

    def to_q(step, other, h):
        p, at = place(step, other), part(h, GRAD_Q_PARTS)
        return sum(dot(cts[square(bits)], weights[square(bits), p, :, at], ((1,), (0,))) for bits in order)

    def to_c(bits):
        k = square(bits)
        return sum(dot(weights[k, p], qs[p], ((1,), (0,))) for p in range(places))

    def q_lanes(h):
        return range(h * lane_tiles // GRAD_Q_PARTS, (h + 1) * lane_tiles // GRAD_Q_PARTS)

    def grad_copy(index, src, dst, device, h=0):
        return remote(src, dst, grad_send.at[index, h], grad_recv.at[index, h], device)

    def g_sib(h):
        return grad_copy(0, out_sib.at[h], in_sib.at[h], sibling, h)

    def g_next():
        return grad_copy(1, out_next, in_next, square_device(NEXT))

    def g_corner(h):
        at = part(h, GRAD_C_PARTS)
        return grad_copy(2, out_corner.at[at, :], in_corner.at[at, :], square_device(NEXT), h)

    def g_over(h):
        at = part(h, GRAD_C_PARTS)
        return grad_copy(3, out_over.at[at, :], in_over.at[at, :], square_device(OVER), h)

    def g_sib_far(step, h):
        return grad_copy(3 + step, out_sib_far.at[step - 1, h], in_sib_far.at[step - 1, h], sibling, h)

    def g_far(step, h):
        return grad_copy(2 + far_count + step, out_far.at[step - 1, h], in_far.at[step - 1, h], far_device(step, 0), h)

    order = (CORNER, NEXT, OVER, 0)
    steps = range(1, far_count)

    def sib_far(step, h):
        out_sib_far[step - 1, h] = to_q(step, 1, h).astype(BF16)
        g_sib_far(step, h).start()

    def far(step, h):
        ours = to_q(step, 0, h)
        g_sib_far(step, h).wait_recv()
        out_far[step - 1, h] = (ours + in_sib_far[step - 1, h].astype(F32)).astype(BF16)
        g_far(step, h).start()

    later = order[1:]
    for step in steps:
        weigh(CORNER, step, 1, all_lanes)
        for bits in later:
            weigh(bits, step, 1, q_lanes(0))
        sib_far(step, 0)
    for step in steps:
        weigh(CORNER, step, 0, all_lanes)
    for other in (0, 1):
        weigh(CORNER, 0, other, all_lanes)
    out_corner[...] = to_c(CORNER).astype(BF16)
    for h in range(GRAD_C_PARTS):
        g_corner(h).start()
    for step in steps:
        for h in range(GRAD_Q_PARTS):
            if h + 1 < GRAD_Q_PARTS:
                for bits in later:
                    weigh(bits, step, 1, q_lanes(h + 1))
                sib_far(step, h + 1)
            for bits in later:
                weigh(bits, step, 0, q_lanes(h))
            far(step, h)
    for other in (0, 1):
        weigh(NEXT, 0, other, all_lanes)
    out_next[...] = to_c(NEXT).astype(BF16)
    g_next().start()
    for other in (0, 1):
        weigh(OVER, 0, other, all_lanes)
    sum_c[0] = to_c(OVER)
    weigh(0, 0, 1, all_lanes)
    for h in range(GRAD_Q_PARTS):
        out_sib[h] = to_q(0, 1, h).astype(BF16)
        g_sib(h).start()
    for h in range(GRAD_C_PARTS):
        at = part(h, GRAD_C_PARTS)
        g_corner(h).wait_recv()
        out_over[at, :] = (sum_c[0, at, :] + in_corner[at, :].astype(F32)).astype(BF16)
        g_over(h).start()
    weigh(0, 0, 0, all_lanes)
    sum_c[1] = to_c(0)
    sum_q = [to_q(0, 0, h) for h in range(GRAD_Q_PARTS)]

    own_values = packed[mine]

    def at_positive(x):
        return spread(total_rows(jnp.where(matches, x, 0.0), jnp.add), jnp.add, lane, outer)[:1]

    positive_score = at_positive(own_values)
    positive_col = at_positive(lses[pl.ds(lse_rows, SUBLANES), :])
    own_row = lses[pl.ds(mine, 1), :]
    per_query_ref[...] = 0.5 * (own_row - positive_score) + 0.5 * (positive_col - positive_score)

    for h in range(GRAD_Q_PARTS):
        g_sib(h).wait_recv()
        total = sum_q[h] + in_sib[h].astype(F32)
        for step in steps:
            g_far(step, h).wait_recv()
            total = total + in_far[step - 1, h].astype(F32)
        wide[0, part(h, GRAD_Q_PARTS), :] = total.T
    for i in range(block):
        out_q[pl.ds(i * length, length), :] = wide[0, pl.ds(i, length, stride=block), :]
    store_q = pltpu.make_async_copy(out_q, grad_q_hbm, local_sem.at[4])
    store_q.start()

    g_next().wait_recv()
    for h in range(GRAD_C_PARTS):
        at = part(h, GRAD_C_PARTS)
        g_over(h).wait_recv()
        wide[1, at, :] = sum_c[1, at, :] + in_next[at, :].astype(F32) + in_over[at, :].astype(F32)
    for j in range(block):
        start = (j // SUBLANES) * SUBLANES * length + j % SUBLANES
        out_c[pl.ds(j * length, length), :] = wide[1, pl.ds(start, length, stride=SUBLANES), :]
    store_c = pltpu.make_async_copy(out_c, grad_c_hbm, local_sem.at[5])
    store_c.start()

    for h in range(C_PARTS):
        for copy in (c_over(h), c_next(h), c_corner(h)):
            copy.wait_send()
    q_sib().wait_send()
    for step in steps:
        for h in range(Q_PARTS):
            q_far(step, h).wait_send()
            q_far_sib(step, h).wait_send()
    for copy in stat_copies:
        copy.wait_send()
    g_next().wait_send()
    for h in range(GRAD_C_PARTS):
        g_corner(h).wait_send()
        g_over(h).wait_send()
    for h in range(GRAD_Q_PARTS):
        g_sib(h).wait_send()
        for step in steps:
            g_sib_far(step, h).wait_send()
            g_far(step, h).wait_send()
    store_q.wait()
    store_c.wait()


def deliver(per_query, grad_q, grad_c, per_query_out, grad_q_out, grad_c_out):
    per_query_out[...] = per_query[:, : per_query_out.shape[1]]
    grad_q_out[...] = grad_q[...]
    grad_c_out[...] = grad_c[...]


def shards(queries, clauses, pattern, positive):
    block, length, width = queries.shape
    tokens = block * length
    far_count = lax.axis_size("row") // SQUARE
    places = 2 * far_count
    far = max(far_count - 1, 1)
    q_piece = (GRAD_Q_PARTS, width, tokens // GRAD_Q_PARTS)
    vmem = pl.BlockSpec(memory_space=pltpu.VMEM)
    hbm = pl.BlockSpec(memory_space=pltpu.HBM)
    sems = pltpu.SemaphoreType.DMA
    V = pltpu.VMEM
    per_query, grad_q, grad_c = pl.pallas_call(
        functools.partial(kernel, (block, length, width), far_count),
        out_shape=(
            jax.ShapeDtypeStruct((1, LANES), F32),
            jax.ShapeDtypeStruct((tokens, width), F32),
            jax.ShapeDtypeStruct((tokens, width), F32),
        ),
        in_specs=[hbm] * 4,
        out_specs=(vmem, hbm, hbm),
        scratch_shapes=[
            V((2, tokens, width), BF16),
            V((2, tokens, width), F32),
            V((places, tokens, width), BF16),
            V((SQUARE, tokens, width), BF16),
            V((SQUARE, width, tokens), BF16),
            V((SQUARE, places, tokens, tokens), F32),
            V((SQUARE, places, block, tokens), F32),
            V((SQUARE, places, block, LANES), F32),
            V((places, SUBLANES, LANES), F32),
            V((places, 2 * places, LANES), F32),
            V((SQUARE, 2 * SUBLANES, LANES), F32),
            V((places + -places % SUBLANES + SUBLANES, LANES), F32),
            V((places, SUBLANES, LANES), F32),
            V((SQUARE, places, tokens, tokens), BF16),
            V((2, tokens, width), F32),
            V((tokens, width), F32),
            V((tokens, width), F32),
        ]
        + [
            V((far, *q_piece), BF16),
            V((far, *q_piece), BF16),
            V((tokens, width), BF16),
            V((tokens, width), BF16),
            V((tokens, width), BF16),
            V(q_piece, BF16),
        ]
        * 2
        + [
            pltpu.SMEM(pattern.shape, jnp.int32),
            pltpu.SMEM(positive.shape, jnp.int32),
            sems((6,)),
            sems((2 * far_count + 2, max(Q_PARTS, C_PARTS))),
            sems((2 * far_count + 2, max(Q_PARTS, C_PARTS))),
            sems((places + SQUARE - 2,)),
            sems((places + SQUARE - 2,)),
            sems((2 * far_count + 2, max(GRAD_Q_PARTS, GRAD_C_PARTS))),
            sems((2 * far_count + 2, max(GRAD_Q_PARTS, GRAD_C_PARTS))),
        ],
        compiler_params=pltpu.CompilerParams(
            collective_id=0, has_side_effects=True, vmem_limit_bytes=60 * 1024 * 1024
        ),
        name="contrastive",
    )(queries.reshape(tokens, width), clauses.reshape(tokens, width), pattern, positive)
    per_query, grad_q, grad_c = pl.pallas_call(
        deliver,
        out_shape=(
            jax.ShapeDtypeStruct((1, block), F32),
            jax.ShapeDtypeStruct((tokens, width), F32),
            jax.ShapeDtypeStruct((tokens, width), F32),
        ),
        in_specs=[vmem] * 3,
        out_specs=(vmem, vmem, vmem),
        name="deliver",
    )(per_query, grad_q, grad_c)
    return (
        per_query.reshape(block),
        grad_q.reshape(queries.shape),
        grad_c.reshape(clauses.shape),
    )


def solution(mesh):
    rows = P(("groups", "row", "col"), None, None)
    ids = P(("groups", "row", "col"))
    return jax.shard_map(
        shards,
        mesh=mesh,
        in_specs=(rows, rows, P("groups", None), ids),
        out_specs=(ids, rows, rows),
        check_vma=False,
    )
```

```python
import functools
import math

import jax
import jax.numpy as jnp
from jax import lax
from jax.experimental import pallas as pl
from jax.experimental.pallas import tpu as pltpu
from jax.sharding import PartitionSpec as P

SHARPNESS = 3.0
FLOOR_VALUE = -1e30
EXP2_SCALE = SHARPNESS * math.log2(math.e)
F32 = jnp.float32
BF16 = jnp.bfloat16
MESH = pl.DeviceIdType.MESH
LANES = 128
SUBLANES = 8
SQUARE = 4
NEXT, OVER, CORNER = 1, 2, 3
Q_PARTS, C_PARTS = 4, 2
GRAD_Q_PARTS, GRAD_C_PARTS = 2, 4


def dot(a, b, dims):
    return lax.dot_general(a, b, (dims, ((), ())), preferred_element_type=F32)


def swap(x, lane, bit):
    return jnp.take_along_axis(x, lane ^ bit, axis=1)


def spread(x, op, lane, bits):
    for bit in bits:
        x = op(x, swap(x, lane, bit))
    return x


def total_rows(x, op):
    for shift in (4, 2, 1):
        x = op(x, pltpu.roll(x, shift, 0))
    return x


def kernel(
    dims, far_count, q_hbm, c_hbm, pattern_hbm, positive_hbm,
    per_query_ref, out_q, out_c,
    stage, wide, qs, cs, cts, raised, inverse, lse_sums, packed, row_stats, col_stats, lses, factors, weights, sum_c,
    out_sib_far, out_far, out_next, out_corner, out_over, out_sib,
    in_sib_far, in_far, in_next, in_corner, in_over, in_sib,
    pattern_ref, positive_ref, local_sem, gather_send, gather_recv, stats_send, stats_recv, grad_send, grad_recv,
):
    block, length, width = dims
    tokens = block * length
    lane_tiles = tokens // LANES
    groups = block // SUBLANES
    places = 2 * far_count
    lse_rows = places + -places % SUBLANES
    row, core = lax.axis_index("row"), lax.axis_index("col")
    a, b = row // SQUARE, row % SQUARE
    mine = a * 2 + core

    def square(bits):
        high, low = b // 2, b % 2
        high = 1 - high if bits & OVER else high
        low = 1 - low if bits & NEXT else low
        return high * 2 + low

    def square_device(bits):
        return {"row": a * SQUARE + square(bits), "col": core}

    def far_row(step):
        return (a + step) % far_count

    def far_device(step, other):
        return {"row": far_row(step) * SQUARE + b, "col": 1 - core if other else core}

    def place(step, other):
        return far_row(step) * 2 + (1 - core if other else core)

    sibling = {"col": 1 - core}
    q_peers = [(step, other) for step in range(far_count) for other in (0, 1) if step or other]
    c_peers = [NEXT, OVER, CORNER]

    def remote(src, dst, send, recv, device):
        return pltpu.make_async_remote_copy(
            src_ref=src, dst_ref=dst, send_sem=send, recv_sem=recv, device_id=device, device_id_type=MESH
        )

    barrier = pltpu.get_barrier_semaphore()
    for step, other in q_peers:
        pl.semaphore_signal(barrier, inc=1, device_id=far_device(step, other), device_id_type=MESH)
    for bits in c_peers:
        pl.semaphore_signal(barrier, inc=1, device_id=square_device(bits), device_id_type=MESH)
    loads = [
        pltpu.make_async_copy(q_hbm, stage.at[0], local_sem.at[0]),
        pltpu.make_async_copy(c_hbm, stage.at[1], local_sem.at[1]),
        pltpu.make_async_copy(pattern_hbm, pattern_ref, local_sem.at[2]),
        pltpu.make_async_copy(positive_hbm, positive_ref, local_sem.at[3]),
    ]
    for load in loads:
        load.start()

    loads[0].wait()
    wide[0] = stage[0].astype(F32)
    for t in range(length):
        qs[mine, pl.ds(t * block, block), :] = wide[0, pl.ds(t, block, stride=length), :].astype(BF16)
    loads[1].wait()
    wide[1] = stage[1].astype(F32)
    for g in range(groups):
        for u in range(0, length, 2):
            pair = [wide[1, pl.ds(g * SUBLANES * length + u + k, SUBLANES, stride=length), :] for k in (0, 1)]
            cs[b, pl.ds((g * length + u) * SUBLANES, 2 * SUBLANES), :] = jnp.concatenate(pair, axis=0).astype(BF16)
    pl.semaphore_wait(barrier, len(q_peers) + len(c_peers))

    def part(h, parts):
        return pl.ds(h * (tokens // parts), tokens // parts)

    def send_c(index, source, bits, h):
        here = cs.at[source, part(h, C_PARTS), :]
        return remote(here, here, gather_send.at[index, h], gather_recv.at[index, h], square_device(bits))

    def send_q(index, source, device, h, parts):
        here = qs.at[source, part(h, parts), :]
        return remote(here, here, gather_send.at[index, h], gather_recv.at[index, h], device)

    def c_over(h):
        return send_c(0, b, OVER, h)

    def c_next(h):
        return send_c(1, b, NEXT, h)

    def c_corner(h):
        return send_c(2, square(OVER), NEXT, h)

    def q_sib():
        return send_q(3, mine, sibling, 0, 1)

    def q_far(step, h):
        return send_q(3 + step, mine, far_device(far_count - step, 0), h, Q_PARTS)

    def q_far_sib(step, h):
        return send_q(2 + far_count + step, place(step, 0), sibling, h, Q_PARTS)

    begun = set()

    def score(name, lanes, gs):
        bits, step, other = name
        c_place, q_place = square(bits), place(step, other)
        for lane in lanes:
            at = pl.ds(lane * LANES, LANES)
            for g in gs:
                rows = pl.ds(g * SUBLANES * length, SUBLANES * length)
                few = pl.ds(g * SUBLANES, SUBLANES)
                logits = dot(cs[c_place, rows, :], qs[q_place, at, :], ((1,), (1,))).reshape(length, SUBLANES, LANES)
                top = jnp.max(logits, axis=0)
                exps = jnp.exp2((logits - top[None]) * EXP2_SCALE)
                total = jnp.sum(exps, axis=0)
                raised[c_place, q_place, rows, at] = exps.reshape(SUBLANES * length, LANES)
                inverse[c_place, q_place, few, at] = 1.0 / total
                lse = top * SHARPNESS + jnp.log(total)
                if (name, g) in begun:
                    lse_sums[c_place, q_place, few, :] += lse
                else:
                    lse_sums[c_place, q_place, few, :] = lse
                    begun.add((name, g))

    all_lanes, all_groups = range(lane_tiles), range(groups)

    def lanes_of(h):
        return range(h * lane_tiles // Q_PARTS, (h + 1) * lane_tiles // Q_PARTS)

    def groups_of(h):
        return range(h * groups // C_PARTS, (h + 1) * groups // C_PARTS)

    for step in range(1, far_count):
        for h in range(Q_PARTS):
            q_far(step, h).start()
    for h in range(C_PARTS):
        c_over(h).start()
    q_sib().start()
    for h in range(C_PARTS):
        c_next(h).start()
    score((0, 0, 0), all_lanes, all_groups)
    cts[b] = cs[b].T

    loads[2].wait()
    loads[3].wait()
    pack_tile = (SUBLANES, LANES)
    lane = lax.broadcasted_iota(jnp.int32, pack_tile, 1)
    sublane = lax.broadcasted_iota(jnp.int32, pack_tile, 0)
    outer = [block << n for n in range(int(math.log2(LANES // block)))]
    inner = [1 << n for n in range(int(math.log2(block)))]

    def scored_lanes(p):
        query_block = ((p // 2) * SQUARE + b) * 2 + p % 2
        flags = jnp.zeros(pack_tile, jnp.int32)
        for k in range(SQUARE):
            first = k * groups * block
            here = (lane >= first) & (lane < first + groups * block)
            flags = jnp.where(here, pattern_ref[query_block, (a * SQUARE + k) * 2 + core], flags)
        return flags > 0

    scored = [scored_lanes(p) for p in range(places)]
    wanted = jnp.full(pack_tile, -1, jnp.int32)
    for i in range(block):
        wanted = jnp.where((lane & (block - 1)) == i, positive_ref[i], wanted)
    wanted = wanted - (row * 2 + core) * block
    for g in range(groups):
        first = (b * groups + g) * block
        here = (lane >= first) & (lane < first + block)
        found = here & (wanted == sublane + g * SUBLANES)
        matches = found if g == 0 else matches | found

    def pack(p):
        parts = [lse_sums[k, p, pl.ds(g * SUBLANES, SUBLANES), :] for k in range(SQUARE) for g in range(groups)]
        bit = LANES // 2
        while len(parts) > 1:
            low = (lane & bit) == 0
            count = len(parts) // 2
            parts = [
                jnp.where(low, x, y) + swap(jnp.where(low, y, x), lane, bit)
                for x, y in zip(parts[:count], parts[count:])
            ]
            bit //= 2
        return parts[0] / SHARPNESS

    q_sib().wait_recv()
    score((0, 0, 1), all_lanes, all_groups)
    for h in range(C_PARTS):
        c_over(h).wait_recv()
        c_corner(h).start()
        for other in (0, 1):
            score((OVER, 0, other), all_lanes, groups_of(h))
        c_next(h).wait_recv()
        for other in (0, 1):
            score((NEXT, 0, other), all_lanes, groups_of(h))
    cts[square(OVER)] = cs[square(OVER)].T
    cts[square(NEXT)] = cs[square(NEXT)].T
    near = (0, OVER, NEXT)
    for step in range(1, far_count):
        for h in range(Q_PARTS + 1):
            if h < Q_PARTS:
                q_far(step, h).wait_recv()
                q_far_sib(step, h).start()
                for bits in near:
                    score((bits, step, 0), lanes_of(h), all_groups)
            if h == Q_PARTS and step == far_count - 1:
                for g in range(C_PARTS - 1):
                    c_corner(g).wait_recv()
                    for s in range(far_count):
                        for other in (0, 1):
                            if s < step or other == 0:
                                score((CORNER, s, other), all_lanes, groups_of(g))
            if h:
                q_far_sib(step, h - 1).wait_recv()
                for bits in near:
                    score((bits, step, 1), lanes_of(h - 1), all_groups)
    for g in range(C_PARTS - 1):
        score((CORNER, far_count - 1, 1), all_lanes, groups_of(g))
    c_corner(C_PARTS - 1).wait_recv()
    for step in range(far_count):
        for other in (0, 1):
            score((CORNER, step, other), all_lanes, groups_of(C_PARTS - 1))

    for p in range(places):
        packed[p] = jnp.where(scored[p], pack(p), FLOOR_VALUE)
    values = [packed[p] for p in range(places)]
    tops, sums = [], []
    for x in values:
        top = spread(total_rows(x, jnp.maximum), jnp.maximum, lane, outer)
        tops.append(top[:1])
        sums.append(spread(total_rows(jnp.exp(x - top), jnp.add), jnp.add, lane, outer)[:1])
    row_stats[mine] = jnp.concatenate(tops + sums, axis=0)

    def send_rows(index, step, other):
        return remote(
            row_stats.at[mine], row_stats.at[mine], stats_send.at[index], stats_recv.at[index], far_device(step, other)
        )

    def send_cols(index, bits):
        return remote(
            col_stats.at[b], col_stats.at[b], stats_send.at[index], stats_recv.at[index], square_device(bits)
        )

    stat_copies = []
    for step, other in q_peers:
        stat_copies.append(send_rows(len(stat_copies), step, other))
        stat_copies[-1].start()
    top = spread(functools.reduce(jnp.maximum, values), jnp.maximum, lane, inner)
    total = spread(sum(jnp.exp(x - top) for x in values), jnp.add, lane, inner)
    col_stats[b] = jnp.concatenate([top, total], axis=0)
    for bits in c_peers:
        stat_copies.append(send_cols(len(stat_copies), bits))
        stat_copies[-1].start()
    cts[square(CORNER)] = cs[square(CORNER)].T
    for copy in stat_copies:
        copy.wait_recv()

    def combine(stats, count, rows):
        top = functools.reduce(jnp.maximum, [stats[s, pl.ds(0, rows), :] for s in range(count)])
        total = sum(
            stats[s, pl.ds(rows, rows), :] * jnp.exp(stats[s, pl.ds(0, rows), :] - top) for s in range(count)
        )
        return top + jnp.log(total)

    row_lse = combine(row_stats, places, places)
    col_lse = combine(col_stats, SQUARE, SUBLANES)
    for p in range(places):
        x = values[p]
        factors[p] = 0.5 * (jnp.exp(x - row_lse[p : p + 1]) + jnp.exp(x - col_lse))
    factors[mine] = factors[mine] - jnp.where(matches, 1.0, 0.0)
    lses[pl.ds(0, places), :] = row_lse
    lses[pl.ds(lse_rows, SUBLANES), :] = col_lse

    def factor_of(k, p, g):
        return jnp.take_along_axis(factors[p], (k * groups + g) * block + (lane & (block - 1)), axis=1)

    weighed = set()

    def weigh(bits, step, other, lanes, gs):
        k, p = square(bits), place(step, other)
        for lane_tile in lanes:
            at = pl.ds(lane_tile * LANES, LANES)
            for g in gs:
                if (bits, step, other, lane_tile, g) in weighed:
                    continue
                weighed.add((bits, step, other, lane_tile, g))
                rows = pl.ds(g * SUBLANES * length, SUBLANES * length)
                few = pl.ds(g * SUBLANES, SUBLANES)
                scale = factor_of(k, p, g) * inverse[k, p, few, at]
                exps = raised[k, p, rows, at].reshape(length, SUBLANES, LANES)
                weights[k, p, rows, at] = (exps * scale[None]).reshape(SUBLANES * length, LANES).astype(BF16)

    def to_q(step, other, h):
        p, at = place(step, other), part(h, GRAD_Q_PARTS)
        for bits in order:
            weigh(bits, step, other, q_lanes(h), all_groups)
        return sum(dot(cts[square(bits)], weights[square(bits), p, :, at], ((1,), (0,))) for bits in order)

    def to_c(bits, g):
        k, rows = square(bits), part(g, groups)
        for step in range(far_count):
            for other in (1, 0):
                weigh(bits, step, other, all_lanes, [g])
        return sum(dot(weights[k, p, rows, :], qs[p], ((1,), (0,))) for p in range(places))

    def q_lanes(h):
        return range(h * lane_tiles // GRAD_Q_PARTS, (h + 1) * lane_tiles // GRAD_Q_PARTS)

    def grad_copy(index, src, dst, device, h=0):
        return remote(src, dst, grad_send.at[index, h], grad_recv.at[index, h], device)

    def g_sib(h):
        return grad_copy(0, out_sib.at[h], in_sib.at[h], sibling, h)

    def g_next():
        return grad_copy(1, out_next, in_next, square_device(NEXT))

    def g_corner(h):
        at = part(h, GRAD_C_PARTS)
        return grad_copy(2, out_corner.at[at, :], in_corner.at[at, :], square_device(NEXT), h)

    def g_over(h):
        at = part(h, GRAD_C_PARTS)
        return grad_copy(3, out_over.at[at, :], in_over.at[at, :], square_device(OVER), h)

    def g_sib_far(step, h):
        return grad_copy(3 + step, out_sib_far.at[step - 1, h], in_sib_far.at[step - 1, h], sibling, h)

    def g_far(step, h):
        return grad_copy(2 + far_count + step, out_far.at[step - 1, h], in_far.at[step - 1, h], far_device(step, 0), h)

    order = (CORNER, NEXT, OVER, 0)
    steps = range(1, far_count)

    def sib_far(step, h):
        out_sib_far[step - 1, h] = to_q(step, 1, h).astype(BF16)
        g_sib_far(step, h).start()

    def far(step, h):
        ours = to_q(step, 0, h)
        g_sib_far(step, h).wait_recv()
        out_far[step - 1, h] = (ours + in_sib_far[step - 1, h].astype(F32)).astype(BF16)
        g_far(step, h).start()

    for step in steps:
        sib_far(step, 0)
    for g in range(groups):
        out_corner[part(g, groups), :] = to_c(CORNER, g).astype(BF16)
        for h in range(g * GRAD_C_PARTS // groups, (g + 1) * GRAD_C_PARTS // groups):
            g_corner(h).start()
    for h in range(1, GRAD_Q_PARTS):
        for step in steps:
            sib_far(step, h)
    for step in steps:
        far(step, 0)
    for g in range(groups):
        sum_c[0, part(g, groups), :] = to_c(OVER, g)
    for h in range(1, GRAD_Q_PARTS):
        for step in steps:
            far(step, h)
    for g in range(groups):
        out_next[part(g, groups), :] = to_c(NEXT, g).astype(BF16)
    g_next().start()
    for h in range(GRAD_Q_PARTS):
        out_sib[h] = to_q(0, 1, h).astype(BF16)
        g_sib(h).start()
    for h in range(GRAD_C_PARTS):
        at = part(h, GRAD_C_PARTS)
        g_corner(h).wait_recv()
        out_over[at, :] = (sum_c[0, at, :] + in_corner[at, :].astype(F32)).astype(BF16)
        g_over(h).start()
    for g in range(groups):
        sum_c[1, part(g, groups), :] = to_c(0, g)
    sum_q = [to_q(0, 0, h) for h in range(GRAD_Q_PARTS)]

    own_values = packed[mine]

    def at_positive(x):
        return spread(total_rows(jnp.where(matches, x, 0.0), jnp.add), jnp.add, lane, outer)[:1]

    positive_score = at_positive(own_values)
    positive_col = at_positive(lses[pl.ds(lse_rows, SUBLANES), :])
    own_row = lses[pl.ds(mine, 1), :]
    per_query_ref[...] = 0.5 * (own_row - positive_score) + 0.5 * (positive_col - positive_score)

    for h in range(GRAD_Q_PARTS):
        g_sib(h).wait_recv()
        total = sum_q[h] + in_sib[h].astype(F32)
        for step in steps:
            g_far(step, h).wait_recv()
            total = total + in_far[step - 1, h].astype(F32)
        wide[0, part(h, GRAD_Q_PARTS), :] = total.T
    for i in range(block):
        out_q[pl.ds(i * length, length), :] = wide[0, pl.ds(i, length, stride=block), :]

    g_next().wait_recv()
    for h in range(GRAD_C_PARTS):
        at = part(h, GRAD_C_PARTS)
        g_over(h).wait_recv()
        wide[1, at, :] = sum_c[1, at, :] + in_next[at, :].astype(F32) + in_over[at, :].astype(F32)
    for j in range(block):
        start = (j // SUBLANES) * SUBLANES * length + j % SUBLANES
        out_c[pl.ds(j * length, length), :] = wide[1, pl.ds(start, length, stride=SUBLANES), :]

    for h in range(C_PARTS):
        for copy in (c_over(h), c_next(h), c_corner(h)):
            copy.wait_send()
    q_sib().wait_send()
    for step in steps:
        for h in range(Q_PARTS):
            q_far(step, h).wait_send()
            q_far_sib(step, h).wait_send()
    for copy in stat_copies:
        copy.wait_send()
    g_next().wait_send()
    for h in range(GRAD_C_PARTS):
        g_corner(h).wait_send()
        g_over(h).wait_send()
    for h in range(GRAD_Q_PARTS):
        g_sib(h).wait_send()
        for step in steps:
            g_sib_far(step, h).wait_send()
            g_far(step, h).wait_send()


def deliver(per_query, grad_q, grad_c, per_query_out, grad_q_out, grad_c_out):
    per_query_out[...] = per_query[:, : per_query_out.shape[1]]
    grad_q_out[...] = grad_q[...]
    grad_c_out[...] = grad_c[...]


def shards(queries, clauses, pattern, positive):
    block, length, width = queries.shape
    tokens = block * length
    far_count = lax.axis_size("row") // SQUARE
    places = 2 * far_count
    far = max(far_count - 1, 1)
    q_piece = (GRAD_Q_PARTS, width, tokens // GRAD_Q_PARTS)
    vmem = pl.BlockSpec(memory_space=pltpu.VMEM)
    hbm = pl.BlockSpec(memory_space=pltpu.HBM)
    sems = pltpu.SemaphoreType.DMA
    V = pltpu.VMEM
    per_query, grad_q, grad_c = pl.pallas_call(
        functools.partial(kernel, (block, length, width), far_count),
        out_shape=(
            jax.ShapeDtypeStruct((1, LANES), F32),
            jax.ShapeDtypeStruct((tokens, width), F32),
            jax.ShapeDtypeStruct((tokens, width), F32),
        ),
        in_specs=[hbm] * 4,
        out_specs=(vmem, vmem, vmem),
        scratch_shapes=[
            V((2, tokens, width), BF16),
            V((2, tokens, width), F32),
            V((places, tokens, width), BF16),
            V((SQUARE, tokens, width), BF16),
            V((SQUARE, width, tokens), BF16),
            V((SQUARE, places, tokens, tokens), F32),
            V((SQUARE, places, block, tokens), F32),
            V((SQUARE, places, block, LANES), F32),
            V((places, SUBLANES, LANES), F32),
            V((places, 2 * places, LANES), F32),
            V((SQUARE, 2 * SUBLANES, LANES), F32),
            V((places + -places % SUBLANES + SUBLANES, LANES), F32),
            V((places, SUBLANES, LANES), F32),
            V((SQUARE, places, tokens, tokens), BF16),
            V((2, tokens, width), F32),
        ]
        + [
            V((far, *q_piece), BF16),
            V((far, *q_piece), BF16),
            V((tokens, width), BF16),
            V((tokens, width), BF16),
            V((tokens, width), BF16),
            V(q_piece, BF16),
        ]
        * 2
        + [
            pltpu.SMEM(pattern.shape, jnp.int32),
            pltpu.SMEM(positive.shape, jnp.int32),
            sems((4,)),
            sems((2 * far_count + 2, max(Q_PARTS, C_PARTS))),
            sems((2 * far_count + 2, max(Q_PARTS, C_PARTS))),
            sems((places + SQUARE - 2,)),
            sems((places + SQUARE - 2,)),
            sems((2 * far_count + 2, max(GRAD_Q_PARTS, GRAD_C_PARTS))),
            sems((2 * far_count + 2, max(GRAD_Q_PARTS, GRAD_C_PARTS))),
        ],
        compiler_params=pltpu.CompilerParams(
            collective_id=0, has_side_effects=True, vmem_limit_bytes=60 * 1024 * 1024
        ),
        name="contrastive",
    )(queries.reshape(tokens, width), clauses.reshape(tokens, width), pattern, positive)
    per_query, grad_q, grad_c = pl.pallas_call(
        deliver,
        out_shape=(
            jax.ShapeDtypeStruct((1, block), F32),
            jax.ShapeDtypeStruct((tokens, width), F32),
            jax.ShapeDtypeStruct((tokens, width), F32),
        ),
        in_specs=[vmem] * 3,
        out_specs=(vmem, vmem, vmem),
        name="deliver",
    )(per_query, grad_q, grad_c)
    return (
        per_query.reshape(block),
        grad_q.reshape(queries.shape),
        grad_c.reshape(clauses.shape),
    )


def solution(mesh):
    rows = P(("groups", "row", "col"), None, None)
    ids = P(("groups", "row", "col"))
    return jax.shard_map(
        shards,
        mesh=mesh,
        in_specs=(rows, rows, P("groups", None), ids),
        out_specs=(ids, rows, rows),
        check_vma=False,
    )
```
